256 devices in a mesh: seq: 16 (over x, y_hi, core), chan: 16 (over y_lo, z).
Axes of the slice: x: 4, y: 4 (y_hi: 2, y_lo: 2; y = y_hi * 2 + y_lo), z: 8, core: 2. Of those that a mesh axis runs over, the one named last changes fastest.
Arguments:
- values: bfloat16 [256, 131072], P('chan', 'seq'), may hold values from -6 to 6
- gate_in: bfloat16 [256, 131072], P('chan', 'seq'), may hold values from -6 to 6
- gate_out: bfloat16 [256, 131072], P('chan', 'seq'), may hold values from -6 to 6
- filters: float32 [256, 131072], P('chan', 'seq'), may hold values from -1.5 to 1.5
- skip_gain: float32 [256], P('chan'), may hold values from 0.5 to 2
- out_proj: bfloat16 [256, 8192], P(None, 'chan'), may hold values from -0.375 to 0.375
Outputs:
- projected: bfloat16 [131072, 8192], P('seq', 'chan')
The draws below stay inside these ranges and needn't reach their ends.
All inputs are finite; a program needn't handle non-finite values.
Results may differ from the reference program's by a relative error of at most 0.0049.
Values may be sent and summed in bfloat16 or wider, within the bound.
A program may use at most 128 MiB of HBM per device.

```python
import math
import jax
import jax.numpy as jnp
from jax import lax

D = 8192
CH_DEV = 16
CONV_CHANNELS = 256
WINDOW_LENGTH = 131072


def draw_filters(key, part):
    random_subkeys = jax.random.split(key, 6)
    steps_float = jnp.arange(WINDOW_LENGTH, dtype=jnp.float32)[None, :]
    integer_steps = jnp.arange(WINDOW_LENGTH, dtype=jnp.int32)[None, :]
    slow_share = 0.5
    slow_flag = jax.random.bernoulli(random_subkeys[0], slow_share, (CONV_CHANNELS, 1))
    slow_rate = jnp.exp(jax.random.uniform(random_subkeys[1], (CONV_CHANNELS, 1), jnp.float32, jnp.log(0.2 / WINDOW_LENGTH), jnp.log(2.0 / WINDOW_LENGTH)))
    fast_rate = jnp.exp(jax.random.uniform(random_subkeys[2], (CONV_CHANNELS, 1), jnp.float32, jnp.log(1.0 / 50.0), jnp.log(1.0 / 30.0)))
    rates = jnp.where(slow_flag, slow_rate, fast_rate)
    decay_profile = jnp.exp(-rates * steps_float)
    spike_location = jax.random.randint(random_subkeys[3], (CONV_CHANNELS, 3), 0, WINDOW_LENGTH)
    spike_falloff = jax.random.uniform(random_subkeys[4], (CONV_CHANNELS, 3), jnp.float32, 0.2, 0.5)
    for selected_choice in range(3):
        decay_profile = decay_profile * jnp.where(integer_steps >= spike_location[:, selected_choice:selected_choice + 1], 1.0 - spike_falloff[:, selected_choice:selected_choice + 1], 1.0)
    scaling = jnp.sqrt(jnp.expm1(-2.0 * rates) / jnp.expm1(-2.0 * rates * WINDOW_LENGTH))
    noise = jax.random.truncated_normal(random_subkeys[5], -4.0, 4.0, (CONV_CHANNELS, WINDOW_LENGTH), jnp.float32)
    return (noise * decay_profile * scaling).astype(jnp.float32)


def levels(stream_key, extent, cuts, least, high):
    gain, own = 1.0, jax.random.fold_in(stream_key, 6)
    for dim, blocks in cuts:
        steps = jnp.exp(jax.random.uniform(jax.random.fold_in(own, dim), (blocks,), jnp.float32, least / len(cuts), high / len(cuts)))
        gain = gain * jnp.repeat(steps, extent[dim] // blocks).reshape([-1 if axis == dim else 1 for axis in range(len(extent))])
    return gain


def gaussian(stream_key, extent, width, most, cuts=(), kind=jnp.bfloat16):
    drawn = width * jax.random.normal(stream_key, extent, jnp.float32)
    if cuts:
        drawn = drawn * levels(stream_key, extent, cuts, -0.22, 0.18)
    return jnp.clip(drawn, -most, most).astype(kind)


def setup_inputs(seed: int = 0) -> dict:
    seeds = jax.random.split(jax.random.key(seed), 7)
    values = gaussian(seeds[0], (CONV_CHANNELS, WINDOW_LENGTH), 1.0, 6.0, ((0, 16), (1, 16)))
    gate_in = gaussian(seeds[1], (CONV_CHANNELS, WINDOW_LENGTH), 1.0, 6.0, ((0, 16), (1, 16)))
    gate_out = gaussian(seeds[2], (CONV_CHANNELS, WINDOW_LENGTH), 1.0, 6.0, ((0, 16), (1, 16)))
    filters = draw_filters(jax.random.fold_in(seeds[6], 71), 0)
    skip_gain = jnp.clip(jnp.exp(math.log(2.0) - 1.3862944 * jax.random.uniform(seeds[4], (CONV_CHANNELS,), jnp.float32) ** levels(seeds[4], (CONV_CHANNELS,), ((0, 16),), -0.2, 0.2)), 0.5, 2.0)
    out_proj = gaussian(seeds[5], (CONV_CHANNELS, D), CONV_CHANNELS ** -0.5, 0.375, ((1, 16),))
    return dict(values=values, gate_in=gate_in, gate_out=gate_out, filters=filters, skip_gain=skip_gain, out_proj=out_proj)


def reference(values, gate_in, gate_out, filters, skip_gain, out_proj):
    mixed_in = values.astype(jnp.float32) * gate_in.astype(jnp.float32)
    operands = (mixed_in.reshape(CONV_CHANNELS // CH_DEV, CH_DEV, WINDOW_LENGTH), filters.reshape(CONV_CHANNELS // CH_DEV, CH_DEV, WINDOW_LENGTH))

    def convolve(group):
        spectrum = jnp.fft.rfft(group[0], n=2 * WINDOW_LENGTH, axis=-1) * jnp.fft.rfft(group[1], n=2 * WINDOW_LENGTH, axis=-1)
        return jnp.fft.irfft(spectrum, n=2 * WINDOW_LENGTH, axis=-1)[:, :WINDOW_LENGTH]

    convolved = lax.map(convolve, operands).reshape(CONV_CHANNELS, WINDOW_LENGTH).astype(jnp.float32)
    gated_out = (gate_out.astype(jnp.float32) * (convolved + skip_gain[:, None] * mixed_in)).astype(jnp.bfloat16)
    return jnp.dot(gated_out.T, out_proj, preferred_element_type=jnp.float32).astype(jnp.bfloat16)
```

```python
import functools
import math

import jax
import jax.numpy as jnp
import numpy as np
from jax import lax
from jax.experimental import pallas as pl
from jax.experimental.pallas import tpu as pltpu
from jax.sharding import PartitionSpec as P

MESH = pl.DeviceIdType.MESH
F32, BF16 = jnp.float32, jnp.bfloat16
SEQ, CHAN = 16, 16
LANES = 128
ROWS = 64
TOTAL = SEQ * ROWS
PERIOD = 2 * TOTAL * LANES
VM = pl.BlockSpec(memory_space=pltpu.VMEM)
ANY = pl.BlockSpec(memory_space=pl.ANY)


def split_np(table):
    high = table.astype(np.float32).astype(BF16)
    low = (table - high.astype(np.float64)).astype(np.float32).astype(BF16)
    return high, low


def make_tables():
    idx = np.arange(128)
    angle = 2.0 * math.pi / 128 * (idx[:, None] * idx[None, :] % 128)
    c, s = np.cos(angle), np.sin(angle)
    a = np.block([[c, s], [-s, c]])
    hi, lo = split_np(a)
    left_a = np.concatenate([hi, hi, lo], axis=1)
    right_a = np.concatenate([hi, hi, lo], axis=0)
    hi, lo = split_np(np.ascontiguousarray(a.T))
    left_t = np.concatenate([hi, hi, lo], axis=1)
    right_t = np.concatenate([hi, hi, lo], axis=0)
    pos = idx[:, None] * 128 + idx[None, :]
    ang1 = 2.0 * math.pi / PERIOD * pos
    ang2 = 2.0 * math.pi / 16384 * (idx[:, None] * idx[None, :])
    tw = np.stack([np.cos(ang1), np.sin(ang1), np.cos(ang2), np.sin(ang2)]).astype(np.float32)
    return left_a, right_a, left_t, right_t, tw


def prepare_kernel(v_ref, gi_ref, go_ref, mixed_ref, gate_ref, tmp):
    for j in range(ROWS):
        cols = slice(j * LANES, (j + 1) * LANES)
        mixed_ref[pl.ds(j, 16, stride=ROWS), :] = v_ref[:, cols].astype(F32) * gi_ref[:, cols].astype(F32)
        tmp[pl.ds(j, 16, stride=ROWS), :] = go_ref[:, cols].astype(F32)
    gate_ref[...] = tmp[...].astype(BF16)


def prepare(values, gate_in, gate_out):
    return pl.pallas_call(
        prepare_kernel,
        out_shape=(
            jax.ShapeDtypeStruct((TOTAL, LANES), F32),
            jax.ShapeDtypeStruct((TOTAL, LANES), BF16),
        ),
        in_specs=[VM] * 3,
        out_specs=(VM, VM),
        scratch_shapes=[pltpu.VMEM((TOTAL, LANES), F32)],
    )(values, gate_in, gate_out)


def exchange_kernel(mixed, gate, filt, x_ref, g_ref, h_ref, send, recv, local):
    s, k = lax.axis_index("seq"), lax.axis_index("chan")
    barrier = pltpu.get_barrier_semaphore()
    for d in range(1, SEQ):
        pl.semaphore_signal(barrier, inc=1, device_id=(lax.rem(s + d, SEQ), k), device_id_type=MESH)
    pl.semaphore_wait(barrier, SEQ - 1)
    here = pl.ds(pl.multiple_of(s * ROWS, ROWS), ROWS)
    copies = []
    for i, (src, dst) in enumerate(((filt, h_ref), (mixed, x_ref), (gate, g_ref))):
        for d in range(1, SEQ):
            t = lax.rem(s + d, SEQ)
            there = pl.ds(pl.multiple_of(t * ROWS, ROWS), ROWS)
            part = src.at[t // 8, :, lax.rem(t, 8), :] if i == 0 else src.at[there, :]
            copy = pltpu.make_async_remote_copy(
                src_ref=part,
                dst_ref=dst.at[here, :],
                send_sem=send.at[i, d],
                recv_sem=recv.at[i, d],
                device_id=(t, k),
                device_id_type=MESH,
            )
            copy.start()
            copies.append(copy)
        part = src.at[s // 8, :, lax.rem(s, 8), :] if i == 0 else src.at[here, :]
        own = pltpu.make_async_copy(part, dst.at[here, :], local.at[i])
        own.start()
        copies.append(own)
    for copy in copies:
        copy.wait()


def exchange(mixed, gate, filt):
    return pl.pallas_call(
        exchange_kernel,
        out_shape=(
            jax.ShapeDtypeStruct((TOTAL, LANES), F32),
            jax.ShapeDtypeStruct((TOTAL, LANES), BF16),
            jax.ShapeDtypeStruct((TOTAL, LANES), F32),
        ),
        in_specs=[VM, VM, VM],
        out_specs=(VM, VM, VM),
        scratch_shapes=[
            pltpu.SemaphoreType.DMA((3, SEQ)),
            pltpu.SemaphoreType.DMA((3, SEQ)),
            pltpu.SemaphoreType.DMA((3,)),
        ],
        compiler_params=pltpu.CompilerParams(collective_id=0, has_side_effects=True),
    )(mixed, gate, filt)


def half_dft(x):
    r = math.sqrt(0.5)

    def quarter(x0, x1, x2, x3):
        p, q = (x1 - x3) * r, (x1 + x3) * r
        return [
            (x0 + x1 + x2 + x3, None),
            (x0 + p, -(x2 + q)),
            (x0 - x2, x3 - x1),
            (x0 - p, x2 - q),
            (x0 - x1 + x2 - x3, None),
        ]

    even, odd = quarter(x[0], x[2], x[4], x[6]), quarter(x[1], x[3], x[5], x[7])
    bins = [None] * 9
    bins[0] = (even[0][0] + odd[0][0], None)
    bins[8] = (even[0][0] - odd[0][0], None)
    for k in (1, 2, 3):
        c, s = math.cos(2 * math.pi * k / 16), math.sin(2 * math.pi * k / 16)
        orr, oi = odd[k]
        pr, pi = orr * c + oi * s, oi * c - orr * s
        er, ei = even[k]
        bins[k] = (er + pr, ei + pi)
        bins[8 - k] = (er - pr, pi - ei)
    bins[4] = (even[4][0], -odd[4][0])
    return bins


def split(x):
    high = x.astype(BF16)
    return high, (x - high.astype(F32)).astype(BF16)


def dot(a, b):
    return lax.dot_general(a, b, (((1,), (0,)), ((), ())), preferred_element_type=F32)


def conv_kernel(skip_ref, x_ref, h_ref, g_ref, la, ra, lt, rt, tw, o_ref, spec, back, pw):
    chunk = 8

    @pl.loop(0, 128 // chunk)
    def _(i):
        rows = pl.ds(pl.multiple_of(i * chunk, chunk), chunk)
        t1r, t1i = tw[0, rows, :], -tw[1, rows, :]
        powers = [None, (t1r, t1i)]
        for k in range(2, 9):
            ar, ai = powers[k // 2]
            br, bi = powers[k - k // 2]
            powers.append((ar * br - ai * bi, ar * bi + ai * br))
        for k in range(1, 9):
            pw[k - 1, 0, rows, :] = powers[k][0]
            pw[k - 1, 1, rows, :] = powers[k][1]
        for n, ref in enumerate((x_ref, h_ref)):
            cols = pl.ds(n * 128, 128)
            slabs = [ref[pl.ds(pl.multiple_of(a * 128 + i * chunk, chunk), chunk), :] for a in range(8)]
            bins = half_dft(slabs)
            for k in range(9):
                re, im = bins[k]
                if k == 0:
                    im = jnp.zeros_like(re)
                else:
                    pr, pi = powers[k]
                    re, im = (re * pr, re * pi) if im is None else (re * pr - im * pi, re * pi + im * pr)
                spec[k, rows, cols] = re
                spec[k, pl.ds(pl.multiple_of(128 + i * chunk, chunk), chunk), cols] = im

    @pl.loop(0, 9)
    def _(k):
        hi, lo = split(spec[k])
        u = dot(la[...], jnp.concatenate([hi, lo, hi], axis=0))
        t2r, t2i = tw[2], -tw[3]
        both = []
        for n in range(2):
            ur, ui = u[:128, n * 128 : (n + 1) * 128], u[128:, n * 128 : (n + 1) * 128]
            both.append(jnp.concatenate([ur * t2r - ui * t2i, ur * t2i + ui * t2r], axis=1))
        hi, lo = split(jnp.concatenate(both, axis=0))
        v = dot(jnp.concatenate([hi, lo, hi], axis=1), rt[...])
        xr, xi, hr, him = v[:128, :128], v[:128, 128:], v[128:, :128], v[128:, 128:]
        edge = jnp.logical_or(k == 0, k == 8)
        scale = jnp.where(edge, F32(1.0 / PERIOD), F32(2.0 / PERIOD))
        prod = jnp.concatenate([(xr * hr - xi * him) * scale, (xr * him + xi * hr) * scale], axis=1)
        hi, lo = split(prod)
        q = dot(jnp.concatenate([hi, lo, hi], axis=1), ra[...])
        qr, qi = q[:, :128], q[:, 128:]
        hi, lo = split(jnp.concatenate([qr * t2r + qi * t2i, qi * t2r - qr * t2i], axis=0))
        r = dot(lt[...], jnp.concatenate([hi, lo, hi], axis=0))
        back[k] = r

    skip = skip_ref[lax.axis_index("seq")]

    @pl.loop(0, 128 // chunk)
    def _(i):
        rows = pl.ds(pl.multiple_of(i * chunk, chunk), chunk)
        lower = pl.ds(pl.multiple_of(128 + i * chunk, chunk), chunk)
        terms = [(back[0, rows, :], None)]
        for k in range(1, 9):
            re, im = back[k, rows, :], back[k, lower, :]
            pr, pi = pw[k - 1, 0, rows, :], pw[k - 1, 1, rows, :]
            terms.append((re * pr + im * pi, im * pr - re * pi))
        for a in range(8):
            total = terms[0][0] + terms[8][0] * (1.0 if a % 2 == 0 else -1.0)
            for k in range(1, 8):
                c, s = math.cos(2 * math.pi * a * k / 16), math.sin(2 * math.pi * a * k / 16)
                total = total + terms[k][0] * c - terms[k][1] * s
            where = pl.ds(pl.multiple_of(a * 128 + i * chunk, chunk), chunk)
            gated = g_ref[where, :].astype(F32) * (total + skip * x_ref[where, :])
            o_ref[where, :] = gated.astype(BF16).astype(F32)


def convolve(skip, x, h, g, tables):
    return pl.pallas_call(
        conv_kernel,
        out_shape=jax.ShapeDtypeStruct((TOTAL, LANES), F32),
        in_specs=[pl.BlockSpec(memory_space=pltpu.SMEM)] + [VM] * 8,
        out_specs=VM,
        scratch_shapes=[
            pltpu.VMEM((9, 256, 256), F32),
            pltpu.VMEM((9, 256, 128), F32),
            pltpu.VMEM((8, 2, 128, 128), F32),
        ],
    )(skip, x, h, g, *tables)


def gather_kernel(part, full, block, shard, asend, arecv, send, recv, ysend, yrecv, local):
    s, k = lax.axis_index("seq"), lax.axis_index("chan")
    y, z = k // 8, lax.rem(k, 8)
    right = (s, y * 8 + lax.rem(z + 1, 8))
    left = (s, y * 8 + lax.rem(z + 7, 8))
    across = (s, lax.rem(k + 8, 16))

    barrier = pltpu.get_barrier_semaphore()
    for d in range(1, SEQ):
        pl.semaphore_signal(barrier, inc=1, device_id=(lax.rem(s + d, SEQ), k), device_id_type=MESH)
    for t in (right, left, across):
        pl.semaphore_signal(barrier, inc=1, device_id=t, device_id_type=MESH)
    pl.semaphore_wait(barrier, SEQ + 2)

    copies = []
    for d in range(1, SEQ):
        t = lax.rem(s + d, SEQ)
        copy = pltpu.make_async_remote_copy(
            src_ref=part.at[pl.ds(pl.multiple_of(t * ROWS, ROWS), ROWS), :],
            dst_ref=block.at[s // 8, :, lax.rem(s, 8), :],
            send_sem=asend.at[d],
            recv_sem=arecv.at[d],
            device_id=(t, k),
            device_id_type=MESH,
        )
        copy.start()
        copies.append(copy)
    own = pltpu.make_async_copy(
        part.at[pl.ds(pl.multiple_of(s * ROWS, ROWS), ROWS), :],
        block.at[s // 8, :, lax.rem(s, 8), :],
        local.at[0],
    )
    own.start()
    own.wait()
    for copy in copies:
        copy.wait()
    for j in range(ROWS):
        rows = jnp.concatenate([block[0, j], block[1, j]], axis=0)
        shard[:, j * LANES : (j + 1) * LANES] = rows.astype(BF16)

    width = shard.shape[1]
    half, quarter = width // 2, width // 4
    columns = {"a": (0, half), "b": (half, half)}

    def slot(yy, zz, first, size):
        row = pl.multiple_of((yy * 8 + zz) * 16, 16)
        return full.at[pl.ds(row, 16), pl.ds(first, size)]

    pending = []

    def push(src, yy, zz, first, size, target, sems, index):
        copy = pltpu.make_async_remote_copy(
            src_ref=src,
            dst_ref=slot(yy, zz, first, size),
            send_sem=sems[0].at[index],
            recv_sem=sems[1].at[index],
            device_id=target,
            device_id_type=MESH,
        )
        copy.start()
        pending.append(copy)
        return copy

    zsems, ysems = (send, recv), (ysend, yrecv)
    first_half = shard.at[:, pl.ds(0, half)]
    second_half = shard.at[:, pl.ds(half, half)]
    keep = pltpu.make_async_copy(shard, slot(y, z, 0, width), local.at[0])
    keep.start()
    swap = push(first_half, y, z, 0, half, across, ysems, 0)
    flight = {}
    for stream, src, first in ((0, first_half, 0), (1, second_half, half)):
        for way, target in ((0, right), (1, left)):
            flight[stream, way] = push(src, y, z, first, half, target, zsems, stream * 8 + way * 4)
    push(second_half, y, z, half, half, across, ysems, 1)
    swap.wait_recv()
    other = 1 - y
    for way, target in ((0, right), (1, left)):
        flight[2, way] = push(slot(other, z, 0, half), other, z, 0, half, target, zsems, 16 + way * 4)
    waited = [swap]
    for step in range(1, 5):
        for stream in (0, 1, 2):
            owner_y = other if stream == 2 else y
            base = half if stream == 1 else 0
            for way, target in ((0, right), (1, left)):
                copy = flight[stream, way]
                copy.wait_recv()
                waited.append(copy)
                zz = lax.rem(z + 8 - step, 8) if way == 0 else lax.rem(z + step, 8)
                if step < 3:
                    first, size = base, half
                else:
                    first, size = base + way * quarter, quarter
                if step < 4:
                    flight[stream, way] = push(
                        slot(owner_y, zz, first, size), owner_y, zz, first, size, target, zsems,
                        stream * 8 + way * 4 + step,
                    )
                if stream == 1:
                    if step < 4:
                        first, size = base, half
                    push(slot(y, zz, first, size), y, zz, first, size, across, ysems, 2 + way * 4 + step - 1)
    keep.wait()
    for copy in pending:
        copy.wait_send()
    for copy in pending:
        if not any(copy is w for w in waited):
            copy.wait_recv()


def gather(part):
    return pl.pallas_call(
        gather_kernel,
        out_shape=jax.ShapeDtypeStruct((256, ROWS * LANES), BF16),
        in_specs=[VM],
        out_specs=ANY,
        scratch_shapes=[
            pltpu.VMEM((2, ROWS, 8, LANES), F32),
            pltpu.VMEM((16, ROWS * LANES), BF16),
            pltpu.SemaphoreType.DMA((SEQ,)),
            pltpu.SemaphoreType.DMA((SEQ,)),
            pltpu.SemaphoreType.DMA((24,)),
            pltpu.SemaphoreType.DMA((24,)),
            pltpu.SemaphoreType.DMA((10,)),
            pltpu.SemaphoreType.DMA((10,)),
            pltpu.SemaphoreType.DMA((1,)),
        ],
        compiler_params=pltpu.CompilerParams(collective_id=1, has_side_effects=True),
    )(part)


def project_kernel(g_ref, w_ref, o_ref):
    o_ref[...] = lax.dot_general(
        g_ref[...], w_ref[...], (((0,), (0,)), ((), ())), preferred_element_type=F32
    ).astype(BF16)


def project(rows, weights):
    depth, width = weights.shape
    samples = rows.shape[1]
    tile = 512
    return pl.pallas_call(
        project_kernel,
        out_shape=jax.ShapeDtypeStruct((samples, width), BF16),
        grid=(samples // tile,),
        in_specs=[
            pl.BlockSpec((depth, tile), lambda i: (0, i)),
            pl.BlockSpec((depth, width), lambda i: (0, 0)),
        ],
        out_specs=pl.BlockSpec((tile, width), lambda i: (i, 0)),
    )(rows, weights)


def body(tables, values, gate_in, gate_out, filters, skip_gain, out_proj):
    mixed, gate = prepare(values, gate_in, gate_out)
    filt = filters.reshape(2, 8, ROWS, LANES).transpose(0, 2, 1, 3)
    x, g, h = exchange(mixed, gate, filt)
    part = convolve(skip_gain, x, h, g, tables)
    rows = gather(part)
    return project(rows, out_proj)


def solution(mesh):
    placed = (
        P("chan", "seq"),
        P("chan", "seq"),
        P("chan", "seq"),
        P("chan", "seq"),
        P("chan"),
        P(None, "chan"),
    )
    return jax.shard_map(
        functools.partial(body, make_tables()),
        mesh=mesh,
        in_specs=placed,
        out_specs=P("seq", "chan"),
        check_vma=False,
    )
```
